32 devices in a mesh: shell: 4 (over x, core), sky: 8 (over z, y).
Axes of the slice: x: 2, y: 2, z: 4, core: 2. Of those that a mesh axis runs over, the one named last changes fastest.
Arguments:
- coords: int32 [3, 4, 8, 512], P(None, 'shell', 'sky'), may hold values from 0 to 2047, as said below
- weights: bfloat16 [4, 8, 512], P('shell', 'sky'), may hold values from 0.5 to 2
- live: int32 [4, 8], P('shell', 'sky'), may hold values from 128 to 512, as said below
Outputs:
- jackknife: float32 [4, 64, 600], P('shell', 'sky')
The draws below stay inside these ranges and needn't reach their ends.
Inputs may be any that keep to these rules, and one draw needn't show every extreme that they name: On device (a, b), coords[0] lies in [a * 256, (a+1) * 256), coords[1] in [b * 256, (b+1) * 256), coords[2] in [0, 1024). `live`: live slots are the first ones of a device; some device is full in every draw.
All inputs are finite; a program needn't handle non-finite values.
Results may differ from the reference program's by a relative error of at most 0.0003.
Values sent between devices are 32-bit elements; how exact they have to be, the bound alone decides.
A program may use at most 64 MiB of HBM per device.

```python
import math
import jax
import jax.numpy as jnp
from jax import lax

PART_DEV = 512
SIDE_CELLS = 256
SPAN_CELLS = 1024
SUBREGIONS = 8
S_BINS = 30
MU_BINS = 20
SHELL_COUNT = 4
PATCH_COUNT = 8
N_SHELL = 4
N_SKY = 8


def draw_coords(key, part):
    keys = jax.random.split(key, 3)
    shape = (SHELL_COUNT, PATCH_COUNT, PART_DEV)
    radial = jax.random.randint(keys[0], shape, 0, SIDE_CELLS) + lax.broadcasted_iota(jnp.int32, shape, 0) * SIDE_CELLS
    across = jax.random.randint(keys[1], shape, 0, SIDE_CELLS) + lax.broadcasted_iota(jnp.int32, shape, 1) * SIDE_CELLS
    depth = jax.random.randint(keys[2], shape, 0, SPAN_CELLS)
    return jnp.stack([radial, across, depth]).astype(jnp.int32)


def draw_live(key, part):
    keys = jax.random.split(key, 2)
    devices = SHELL_COUNT * PATCH_COUNT
    upper = PART_DEV * 3 // 4
    spread = jax.random.randint(keys[0], (devices,), 0, upper + 1)
    counts = PART_DEV // 4 + spread * spread // max(upper, 1)
    chosen = jax.random.randint(keys[1], (), 0, devices)
    counts = jnp.where(jnp.arange(devices) == chosen, PART_DEV, counts)
    return counts.reshape(SHELL_COUNT, PATCH_COUNT).astype(jnp.int32)


def shard_levels(own_key, dims, cuts, least, high):
    factor_of, own = 1.0, jax.random.fold_in(own_key, 6)
    for dim, parts in cuts:
        steps = jnp.exp(jax.random.uniform(jax.random.fold_in(own, dim), (parts,), jnp.float32, least / len(cuts), high / len(cuts)))
        factor_of = factor_of * jnp.repeat(steps, dims[dim] // parts).reshape([-1 if axis == dim else 1 for axis in range(len(dims))])
    return factor_of


def setup_inputs(seed: int = 0) -> dict:
    arg_keys = jax.random.split(jax.random.key(seed), 4)
    return {
        "coords": draw_coords(jax.random.fold_in(arg_keys[3], 71), 0),
        "weights": jnp.clip(jnp.exp(math.log(2.0) - 1.3862944 * jax.random.uniform(arg_keys[1], (SHELL_COUNT, PATCH_COUNT, PART_DEV), jnp.float32) ** shard_levels(arg_keys[1], (SHELL_COUNT, PATCH_COUNT, PART_DEV), ((0, 4), (1, 8)), -0.2, 0.2)), 0.5, 2.0).astype(jnp.bfloat16),
        "live": draw_live(jax.random.fold_in(arg_keys[3], 71), 0),
    }


def edge_values():
    return [int(4.0 * 10.0 ** (4.0 * level / S_BINS) + 0.5) for level in range(S_BINS + 1)]


def bin_scale(patches):
    edges = edge_values()
    factor = SIDE_CELLS * SIDE_CELLS * SPAN_CELLS / (patches * PART_DEV * PART_DEV)
    values = []
    for level in range(S_BINS):
        volume = (4.0 * math.pi / 3.0) * (edges[level + 1] ** 1.5 - edges[level] ** 1.5) / MU_BINS
        values = values + [factor / volume] * MU_BINS
    return jnp.asarray(values, dtype=jnp.float32)


def pair_counts(own_pos, own_weight, far_pos, far_weight):
    edges = edge_values()
    radial_gap = jnp.minimum(jnp.abs(own_pos[0][:, None] - far_pos[0][None, :]), 255)
    across_gap = jnp.minimum(jnp.abs(own_pos[1][:, None] - far_pos[1][None, :]), 255)
    depth_gap = jnp.minimum(jnp.abs(own_pos[2][:, None] - far_pos[2][None, :]), 255)
    squared = radial_gap * radial_gap + across_gap * across_gap + depth_gap * depth_gap
    radial_sq = radial_gap * radial_gap * (MU_BINS * MU_BINS)
    s_index = jnp.zeros_like(squared)
    for level in range(1, S_BINS):
        s_index = s_index + (squared >= edges[level]).astype(jnp.int32)
    mu_index = jnp.zeros_like(squared)
    for level in range(1, MU_BINS):
        mu_index = mu_index + (radial_sq >= level * level * squared).astype(jnp.int32)
    inside = (squared >= edges[0]) & (squared < edges[S_BINS])
    region = own_pos[2] // (SPAN_CELLS // SUBREGIONS)
    segment = jnp.where(inside, region[:, None] * (S_BINS * MU_BINS) + s_index * MU_BINS + mu_index,
                        SUBREGIONS * S_BINS * MU_BINS).astype(jnp.int32)
    pair_weight = own_weight[:, None] * far_weight[None, :]
    totals = jax.ops.segment_sum(pair_weight.reshape(-1), segment.reshape(-1),
                                 num_segments=SUBREGIONS * S_BINS * MU_BINS + 1)
    return totals[:-1]


def reference(coords, weights, live):
    slots = jnp.arange(PART_DEV, dtype=jnp.int32)
    masked = jnp.where(slots[None, None, :] < live[:, :, None], weights.astype(jnp.float32), jnp.float32(0.0))
    pos_padded = jnp.pad(coords, ((0, 0), (1, 1), (1, 1), (0, 0)))
    weight_padded = jnp.pad(masked, ((1, 1), (1, 1), (0, 0)))
    tile_rows = min(256, PART_DEV)
    zero = jnp.int32(0)

    def one_device(flat):
        shell_at = (flat // N_SKY).astype(jnp.int32)
        patch_at = (flat % N_SKY).astype(jnp.int32)
        far_pos = lax.dynamic_slice(pos_padded, (zero, shell_at, patch_at, zero), (3, 3, 3, PART_DEV)).reshape(3, 9 * PART_DEV)
        far_weight = lax.dynamic_slice(weight_padded, (shell_at, patch_at, zero), (3, 3, PART_DEV)).reshape(9 * PART_DEV)
        own_pos = lax.dynamic_slice(coords, (zero, shell_at, patch_at, zero), (3, 1, 1, PART_DEV)).reshape(3, PART_DEV)
        own_weight = lax.dynamic_slice(masked, (shell_at, patch_at, zero), (1, 1, PART_DEV)).reshape(PART_DEV)

        def one_tile(index):
            start = (index * tile_rows).astype(jnp.int32)
            rows_pos = lax.dynamic_slice_in_dim(own_pos, start, tile_rows, 1)
            rows_weight = lax.dynamic_slice_in_dim(own_weight, start, tile_rows, 0)
            return pair_counts(rows_pos, rows_weight, far_pos, far_weight)

        return jnp.sum(lax.map(one_tile, jnp.arange(PART_DEV // tile_rows, dtype=jnp.int32)), axis=0)

    hists = lax.map(one_device, jnp.arange(N_SHELL * N_SKY, dtype=jnp.int32))
    hists = hists.reshape(N_SHELL, N_SKY, SUBREGIONS, S_BINS * MU_BINS)
    totals = jnp.sum(hists, axis=(1, 2))
    leave = totals[:, None, None, :] - hists
    return (leave * bin_scale(N_SKY)).reshape(N_SHELL, N_SKY * SUBREGIONS, S_BINS * MU_BINS)
```

```python
import math

import jax
import jax.numpy as jnp
from jax import lax
from jax.experimental import pallas as pl
from jax.experimental.pallas import tpu as pltpu
from jax.sharding import PartitionSpec as P

PART_DEV = 512
SIDE_CELLS = 256
SPAN_CELLS = 1024
SUBREGIONS = 8
S_BINS = 30
MU_BINS = 20
LANES = 128
ROWS = 8
UNROLL = 2
BIG = 1.0e6
NT = (((1,), (1,)), ((), ()))


def edge_values():
    return [int(4.0 * 10.0 ** (4.0 * level / S_BINS) + 0.5) for level in range(S_BINS + 1)]


REACH = math.isqrt(edge_values()[S_BINS] - 1)


def bin_scale(patches):
    edges = edge_values()
    factor = SIDE_CELLS * SIDE_CELLS * SPAN_CELLS / (patches * PART_DEV * PART_DEV)
    values = []
    for level in range(S_BINS):
        volume = 4.0 * math.pi / 3.0 * (edges[level + 1] ** 1.5 - edges[level] ** 1.5) / MU_BINS
        values = values + [factor / volume] * MU_BINS
    return jnp.asarray(values, dtype=jnp.float32)


def shifted(block, axis):
    count = lax.axis_size(axis)
    forward = [(i, i + 1) for i in range(count - 1)]
    backward = [(target, source) for source, target in forward]
    return lax.ppermute(block, axis, forward), lax.ppermute(block, axis, backward)


def iota_f(shape, dim):
    return lax.broadcasted_iota(jnp.int32, shape, dim).astype(jnp.float32)


def split_rows(x, y, z, w):
    xh, yh, zh = jnp.floor(x * (1 / 64)), jnp.floor(y * (1 / 64)), jnp.floor(z * (1 / 64))
    rows = [xh, yh, zh, w, x - 64 * xh, y - 64 * yh, z - 64 * zh, jnp.where(w > 0, 1.0, 0.0)]
    rows = rows + [jnp.zeros_like(x)] * 8
    return jnp.concatenate(rows, axis=0).astype(jnp.bfloat16)


def prep_kernel(tri_ref, far_ref, own_ref, meta_ref, cols, ocols):
    total = tri_ref.shape[1]
    parts = total // 3
    origin = (lax.axis_index("shell") * SIDE_CELLS).astype(jnp.float32)
    x, y, z, w = (tri_ref[c : c + 1, :] for c in range(4))
    keep = (w > 0) & (x >= origin - REACH) & (x <= origin + (SIDE_CELLS - 1 + REACH))
    wk = jnp.where(keep, w, 0.0)
    key = jnp.where(keep, z, float(SPAN_CELLS)) * total + iota_f((1, total), 1)
    cols[...] = jnp.broadcast_to(key, (8, total)).T

    def count_block(i, rank):
        col = cols[pl.ds(pl.multiple_of(i * LANES, LANES), LANES), 0:1]
        return rank + jnp.sum(jnp.where(col < key, 1.0, 0.0), axis=0, keepdims=True)

    rank = lax.fori_loop(0, total // LANES, count_block, jnp.zeros((1, total), jnp.float32))
    feats = split_rows(x, y, z, wk)

    def place(c, carry):
        dest = iota_f((LANES, total), 0) + (c * LANES).astype(jnp.float32)
        hot = jnp.where(dest == rank, 1.0, 0.0).astype(jnp.bfloat16)
        res = lax.dot_general(feats, hot, NT, preferred_element_type=jnp.float32)
        pos = 64.0 * res[0:3] + res[4:7]
        alive = res[7:8]
        zmin = jnp.min(jnp.where(alive > 0, pos[2:3], BIG), axis=1, keepdims=True)
        zmax = jnp.max(jnp.where(alive > 0, pos[2:3], -BIG), axis=1, keepdims=True)
        some = jnp.max(alive, axis=1, keepdims=True)
        shape = (1, LANES)
        far_ref[c] = jnp.concatenate(
            [pos, res[3:4], jnp.broadcast_to(zmin, shape), jnp.broadcast_to(zmax, shape),
             jnp.broadcast_to(some, shape), alive], axis=0)
        return carry

    lax.fori_loop(0, total // LANES, place, 0)

    mid = slice(parts, 2 * parts)
    x, y, z, w, key = x[:, mid], y[:, mid], z[:, mid], w[:, mid], key[:, mid]
    key_col = cols[parts : 2 * parts, 0:1]
    order = jnp.sum(jnp.where(key_col < key, 1.0, 0.0), axis=0, keepdims=True)
    region = jnp.floor(z * (SUBREGIONS / SPAN_CELLS))
    alive = w > 0
    pos = order
    for r in range(SUBREGIONS - 1):
        count = jnp.sum(jnp.where(alive & (region == r), 1.0, 0.0), axis=1, keepdims=True)
        gap = jnp.floor((count + (ROWS - 1)) * (1 / ROWS)) * ROWS - count
        pos = pos + jnp.where(region > r, gap, 0.0)
    pos = jnp.where(alive, pos, BIG)
    feats = split_rows(x, y, z, w)
    zs = jnp.concatenate([pos, z] + [pos] * 6, axis=0)
    ocols[...] = zs.T

    def place_own(c, carry):
        dest = iota_f((LANES, parts), 0) + (c * LANES).astype(jnp.float32)
        hot = jnp.where(dest == pos, 1.0, 0.0).astype(jnp.bfloat16)
        own_ref[pl.ds(pl.multiple_of(c * LANES, LANES), LANES), :] = lax.dot_general(
            hot, feats, NT, preferred_element_type=jnp.float32)
        return carry

    lax.fori_loop(0, own_ref.shape[0] // LANES, place_own, 0)
    tile = jnp.floor(ocols[:, 0:1] * (1 / ROWS))
    z_col = ocols[:, 1:2]
    mine = tile == iota_f((parts, LANES), 1)
    tmin = jnp.min(jnp.where(mine, z_col, BIG), axis=0, keepdims=True)
    tmax = jnp.max(jnp.where(mine, z_col, -BIG), axis=0, keepdims=True)
    meta_ref[...] = jnp.concatenate([tmin, tmax] + [tmin] * 6, axis=0)


def bins(dx, q):
    per_two = S_BINS / 4.0 * math.log10(2.0)
    cand = jnp.floor(jnp.log2(q) * per_two + (0.5 - 2.0 * per_two))
    edge = jnp.floor(jnp.exp2(cand * (1.0 / per_two) + 2.0) + 0.5)
    s = jnp.where(q < edge, cand - 1.0, cand)
    near = jnp.floor(jnp.abs(dx) * lax.rsqrt(q) * MU_BINS + 0.5)
    m = jnp.where(dx * dx * (MU_BINS * MU_BINS) < near * near * q, near - 1.0, near)
    return s, jnp.minimum(m, MU_BINS - 1.0)


def pair_kernel(far_ref, own_ref, meta_ref, hist_ref, plan_v, plan_s, sem):
    chunks = far_ref.shape[0] - 1
    height = plan_v.shape[0]
    edges = edge_values()
    tmin, tmax = meta_ref[0:1, :], meta_ref[1:2, :]
    slot = lax.broadcasted_iota(jnp.int32, (height, LANES), 0)
    plan = jnp.full((height, LANES), chunks, jnp.int32)
    count = jnp.zeros((1, LANES), jnp.int32)
    for c in range(chunks):
        info = far_ref[c]
        act = (info[4:5] <= tmax + REACH) & (info[5:6] >= tmin - REACH) & (info[6:7] > 0)
        plan = jnp.where((slot == count) & act, c, plan)
        count = count + jnp.where(act, 1, 0)
    region = jnp.clip(jnp.floor(tmin * (SUBREGIONS / SPAN_CELLS)), 0, SUBREGIONS - 1)
    used = jnp.sum(jnp.where(tmin < BIG, 1.0, 0.0), axis=1, keepdims=True)
    plan = jnp.where(slot == height - 1, count, plan)
    plan = jnp.where(slot == height - 2, region.astype(jnp.int32), plan)
    plan = jnp.where(slot == height - 3, used.astype(jnp.int32), plan)
    plan_v[...] = plan
    copy = pltpu.make_async_copy(plan_v, plan_s, sem)
    copy.start()
    hist_ref[...] = jnp.zeros_like(hist_ref)
    copy.wait()

    half = (16, LANES)
    low = iota_f(half, 0).astype(jnp.bfloat16)
    high = (iota_f(half, 0) + 16.0).astype(jnp.bfloat16)
    none = jnp.zeros(half, jnp.bfloat16)

    def add_tile(t, carry):
        own = own_ref[pl.ds(pl.multiple_of(t * ROWS, ROWS), ROWS), :]
        xi = jnp.broadcast_to(own[:, 0:1] * 64.0 + own[:, 4:5], (ROWS, LANES))
        yi = jnp.broadcast_to(own[:, 1:2] * 64.0 + own[:, 5:6], (ROWS, LANES))
        zi = jnp.broadcast_to(own[:, 2:3] * 64.0 + own[:, 6:7], (ROWS, LANES))
        wi = jnp.broadcast_to(own[:, 3:4], (ROWS, LANES))
        wis = [jnp.broadcast_to(wi[i : i + 1], half).astype(jnp.bfloat16) for i in range(ROWS)]

        def add_chunk(p, acc):
            lhs, rhs = [], []
            for u in range(UNROLL):
                info = far_ref[plan_s[p * UNROLL + u, t]]
                dx, dy, dz = xi - info[0:1], yi - info[1:2], zi - info[2:3]
                q = dx * dx + dy * dy + dz * dz
                s, m = bins(dx, q)
                s = jnp.where((q >= edges[0]) & (q < edges[S_BINS]), s, 99.0)
                wj = jnp.broadcast_to(info[3:4], half).astype(jnp.bfloat16)
                for i in range(ROWS):
                    si = jnp.broadcast_to(s[i : i + 1], half).astype(jnp.bfloat16)
                    mi = jnp.broadcast_to(m[i : i + 1], half).astype(jnp.bfloat16)
                    lhs.append(jnp.concatenate(
                        [jnp.where(si == low, wj, none), jnp.where(si == high, wj, none)], axis=0))
                    rhs.append(jnp.concatenate(
                        [jnp.where(mi == low, wis[i], none), jnp.where(mi == high, wis[i], none)],
                        axis=0))
            return acc + lax.dot_general(
                jnp.concatenate(lhs, axis=1), jnp.concatenate(rhs, axis=1), NT,
                preferred_element_type=jnp.float32)

        steps = (plan_s[height - 1, t] + (UNROLL - 1)) // UNROLL
        acc = lax.fori_loop(0, steps, add_chunk, jnp.zeros((32, 32), jnp.float32))
        r = plan_s[height - 2, t]
        hist_ref[r] = hist_ref[r] + acc
        return carry

    lax.fori_loop(0, plan_s[height - 3, 0], add_tile, 0)


def local(coords, weights, live):
    parts = coords.shape[3]
    slots = lax.iota(jnp.int32, parts)
    own_weight = jnp.where(slots < live[0, 0], weights[0, 0].astype(jnp.float32), 0.0)
    packed = jnp.concatenate(
        [coords.reshape(3, parts).astype(jnp.float32), own_weight.reshape(1, parts)], axis=0
    )
    down, up = shifted(packed, "shell")
    tri = jnp.concatenate([down, packed, up], axis=1)
    total = 3 * parts
    chunks = total // LANES
    own_rows = -(-(parts + SUBREGIONS * (ROWS - 1)) // LANES) * LANES
    vmem = pl.BlockSpec(memory_space=pltpu.VMEM)
    far, own, meta = pl.pallas_call(
        prep_kernel,
        out_shape=(
            jax.ShapeDtypeStruct((chunks, 8, LANES), jnp.float32),
            jax.ShapeDtypeStruct((own_rows, 16), jnp.float32),
            jax.ShapeDtypeStruct((8, LANES), jnp.float32),
        ),
        in_specs=[vmem],
        out_specs=(vmem, vmem, vmem),
        scratch_shapes=[pltpu.VMEM((total, 8), jnp.float32), pltpu.VMEM((parts, 8), jnp.float32)],
    )(tri)
    left, right = shifted(far, "sky")
    every = jnp.concatenate(
        [left, far, right, jnp.zeros((1, 8, LANES), jnp.float32)], axis=0
    )
    height = -(-(3 * chunks + UNROLL + 3) // 8) * 8
    hist = pl.pallas_call(
        pair_kernel,
        out_shape=jax.ShapeDtypeStruct((SUBREGIONS, 32, 32), jnp.float32),
        in_specs=[vmem, vmem, vmem],
        out_specs=vmem,
        scratch_shapes=[
            pltpu.VMEM((height, LANES), jnp.int32),
            pltpu.SMEM((height, LANES), jnp.int32),
            pltpu.SemaphoreType.DMA,
        ],
    )(every, own, meta)
    by_region = hist[:, :S_BINS, :MU_BINS].reshape(SUBREGIONS, S_BINS * MU_BINS)
    sums = lax.all_gather(jnp.sum(by_region, axis=0), "sky")
    shell_total = jnp.sum(sums, axis=0)
    scale = bin_scale(lax.axis_size("sky"))
    leave = (shell_total[None, :] - by_region) * scale[None, :]
    return leave.reshape(1, SUBREGIONS, S_BINS * MU_BINS)


def solution(mesh):
    in_specs = (P(None, "shell", "sky", None), P("shell", "sky", None), P("shell", "sky"))
    out_specs = P("shell", "sky", None)
    return jax.shard_map(local, mesh=mesh, in_specs=in_specs, out_specs=out_specs, check_vma=False)
```

```python
import math

import jax
import jax.numpy as jnp
from jax import lax
from jax.experimental import pallas as pl
from jax.experimental.pallas import tpu as pltpu
from jax.sharding import PartitionSpec as P

PART_DEV = 512
SIDE_CELLS = 256
SPAN_CELLS = 1024
SUBREGIONS = 8
S_BINS = 30
MU_BINS = 20
LANES = 128
ROWS = 8
UNROLL = 8
BIG = 1.0e6
NT = (((1,), (1,)), ((), ()))


def edge_values():
    return [int(4.0 * 10.0 ** (4.0 * level / S_BINS) + 0.5) for level in range(S_BINS + 1)]


REACH = math.isqrt(edge_values()[S_BINS] - 1)


def bin_scale(patches):
    edges = edge_values()
    factor = SIDE_CELLS * SIDE_CELLS * SPAN_CELLS / (patches * PART_DEV * PART_DEV)
    values = []
    for level in range(S_BINS):
        volume = 4.0 * math.pi / 3.0 * (edges[level + 1] ** 1.5 - edges[level] ** 1.5) / MU_BINS
        values = values + [factor / volume] * MU_BINS
    return jnp.asarray(values, dtype=jnp.float32)


def shifted(block, axis):
    count = lax.axis_size(axis)
    forward = [(i, i + 1) for i in range(count - 1)]
    backward = [(target, source) for source, target in forward]
    return lax.ppermute(block, axis, forward), lax.ppermute(block, axis, backward)


def iota_f(shape, dim):
    return lax.broadcasted_iota(jnp.int32, shape, dim).astype(jnp.float32)


def split_rows(x, y, z, w):
    xh, yh, zh = jnp.floor(x * (1 / 64)), jnp.floor(y * (1 / 64)), jnp.floor(z * (1 / 64))
    rows = [xh, yh, zh, w, x - 64 * xh, y - 64 * yh, z - 64 * zh, jnp.where(w > 0, 1.0, 0.0)]
    rows = rows + [jnp.zeros_like(x)] * 8
    return jnp.concatenate(rows, axis=0).astype(jnp.bfloat16)


def prep_kernel(tri_ref, far_ref, own_ref, meta_ref, cols, ocols):
    total = tri_ref.shape[1]
    parts = total // 3
    origin = (lax.axis_index("shell") * SIDE_CELLS).astype(jnp.float32)
    x, y, z, w = (tri_ref[c : c + 1, :] for c in range(4))
    keep = (w > 0) & (x >= origin - REACH) & (x <= origin + (SIDE_CELLS - 1 + REACH))
    wk = jnp.where(keep, w, 0.0)
    key = jnp.where(keep, z, float(SPAN_CELLS)) * total + iota_f((1, total), 1)
    cols[...] = jnp.broadcast_to(key, (8, total)).T

    def count_block(i, rank):
        col = cols[pl.ds(pl.multiple_of(i * LANES, LANES), LANES), 0:1]
        return rank + jnp.sum(jnp.where(col < key, 1.0, 0.0), axis=0, keepdims=True)

    rank = lax.fori_loop(0, total // LANES, count_block, jnp.zeros((1, total), jnp.float32))
    feats = split_rows(x, y, z, wk)

    def place(c, carry):
        dest = iota_f((LANES, total), 0) + (c * LANES).astype(jnp.float32)
        hot = jnp.where(dest == rank, 1.0, 0.0).astype(jnp.bfloat16)
        res = lax.dot_general(feats, hot, NT, preferred_element_type=jnp.float32)
        pos = 64.0 * res[0:3] + res[4:7]
        alive = res[7:8]
        zmin = jnp.min(jnp.where(alive > 0, pos[2:3], BIG), axis=1, keepdims=True)
        zmax = jnp.max(jnp.where(alive > 0, pos[2:3], -BIG), axis=1, keepdims=True)
        some = jnp.max(alive, axis=1, keepdims=True)
        shape = (1, LANES)
        far_ref[c] = jnp.concatenate(
            [pos, res[3:4], jnp.broadcast_to(zmin, shape), jnp.broadcast_to(zmax, shape),
             jnp.broadcast_to(some, shape), alive], axis=0)
        return carry

    lax.fori_loop(0, total // LANES, place, 0)

    mid = slice(parts, 2 * parts)
    x, y, z, w, key = x[:, mid], y[:, mid], z[:, mid], w[:, mid], key[:, mid]
    key_col = cols[parts : 2 * parts, 0:1]
    order = jnp.sum(jnp.where(key_col < key, 1.0, 0.0), axis=0, keepdims=True)
    region = jnp.floor(z * (SUBREGIONS / SPAN_CELLS))
    alive = w > 0
    pos = order
    for r in range(SUBREGIONS - 1):
        count = jnp.sum(jnp.where(alive & (region == r), 1.0, 0.0), axis=1, keepdims=True)
        gap = jnp.floor((count + (ROWS - 1)) * (1 / ROWS)) * ROWS - count
        pos = pos + jnp.where(region > r, gap, 0.0)
    pos = jnp.where(alive, pos, BIG)
    feats = split_rows(x, y, z, w)
    zs = jnp.concatenate([pos, z] + [pos] * 6, axis=0)
    ocols[...] = zs.T

    def place_own(c, carry):
        dest = iota_f((LANES, parts), 0) + (c * LANES).astype(jnp.float32)
        hot = jnp.where(dest == pos, 1.0, 0.0).astype(jnp.bfloat16)
        own_ref[pl.ds(pl.multiple_of(c * LANES, LANES), LANES), :] = lax.dot_general(
            hot, feats, NT, preferred_element_type=jnp.float32)
        return carry

    lax.fori_loop(0, own_ref.shape[0] // LANES, place_own, 0)
    tile = jnp.floor(ocols[:, 0:1] * (1 / ROWS))
    z_col = ocols[:, 1:2]
    mine = tile == iota_f((parts, LANES), 1)
    tmin = jnp.min(jnp.where(mine, z_col, BIG), axis=0, keepdims=True)
    tmax = jnp.max(jnp.where(mine, z_col, -BIG), axis=0, keepdims=True)
    meta_ref[...] = jnp.concatenate([tmin, tmax] + [tmin] * 6, axis=0)


def bins(dx, q):
    per_two = S_BINS / 4.0 * math.log10(2.0)
    cand = jnp.floor(jnp.log2(q) * per_two + (0.5 - 2.0 * per_two))
    edge = jnp.floor(jnp.exp2(cand * (1.0 / per_two) + 2.0) + 0.5)
    s = jnp.where(q < edge, cand - 1.0, cand)
    near = jnp.floor(jnp.abs(dx) * lax.rsqrt(q) * MU_BINS + 0.5)
    m = jnp.where(dx * dx * (MU_BINS * MU_BINS) < near * near * q, near - 1.0, near)
    return s, jnp.minimum(m, MU_BINS - 1.0)


def pair_kernel(far_ref, own_ref, meta_ref, hist_ref, plan_v, plan_s, sem):
    chunks = far_ref.shape[0] - 1
    height = plan_v.shape[0]
    edges = edge_values()
    tmin, tmax = meta_ref[0:1, :], meta_ref[1:2, :]
    slot = lax.broadcasted_iota(jnp.int32, (height, LANES), 0)
    plan = jnp.full((height, LANES), chunks, jnp.int32)
    count = jnp.zeros((1, LANES), jnp.int32)
    for c in range(chunks):
        info = far_ref[c]
        act = (info[4:5] <= tmax + REACH) & (info[5:6] >= tmin - REACH) & (info[6:7] > 0)
        plan = jnp.where((slot == count) & act, c, plan)
        count = count + jnp.where(act, 1, 0)
    region = jnp.clip(jnp.floor(tmin * (SUBREGIONS / SPAN_CELLS)), 0, SUBREGIONS - 1)
    used = jnp.sum(jnp.where(tmin < BIG, 1.0, 0.0), axis=1, keepdims=True)
    plan = jnp.where(slot == height - 1, count, plan)
    plan = jnp.where(slot == height - 2, region.astype(jnp.int32), plan)
    plan = jnp.where(slot == height - 3, used.astype(jnp.int32), plan)
    plan_v[...] = plan
    copy = pltpu.make_async_copy(plan_v, plan_s, sem)
    copy.start()
    hist_ref[...] = jnp.zeros_like(hist_ref)
    copy.wait()

    half = (16, LANES)
    low = iota_f(half, 0).astype(jnp.bfloat16)
    high = (iota_f(half, 0) + 16.0).astype(jnp.bfloat16)
    none = jnp.zeros(half, jnp.bfloat16)

    def add_tile(t, carry):
        own = own_ref[pl.ds(pl.multiple_of(t * ROWS, ROWS), ROWS), :]
        xi = jnp.broadcast_to(own[:, 0:1] * 64.0 + own[:, 4:5], (ROWS, LANES))
        yi = jnp.broadcast_to(own[:, 1:2] * 64.0 + own[:, 5:6], (ROWS, LANES))
        zi = jnp.broadcast_to(own[:, 2:3] * 64.0 + own[:, 6:7], (ROWS, LANES))
        wi = jnp.broadcast_to(own[:, 3:4], (ROWS, LANES))
        wis = [jnp.broadcast_to(wi[i : i + 1], half).astype(jnp.bfloat16) for i in range(ROWS)]

        def add_chunk(p, acc):
            lhs, rhs = [], []
            for u in range(UNROLL):
                info = far_ref[plan_s[p * UNROLL + u, t]]
                dx, dy, dz = xi - info[0:1], yi - info[1:2], zi - info[2:3]
                q = dx * dx + dy * dy + dz * dz
                s, m = bins(dx, q)
                s = jnp.where((q >= edges[0]) & (q < edges[S_BINS]), s, 99.0)
                wj = jnp.broadcast_to(info[3:4], half).astype(jnp.bfloat16)
                for i in range(ROWS):
                    si = jnp.broadcast_to(s[i : i + 1], half).astype(jnp.bfloat16)
                    mi = jnp.broadcast_to(m[i : i + 1], half).astype(jnp.bfloat16)
                    lhs.append(jnp.concatenate(
                        [jnp.where(si == low, wj, none), jnp.where(si == high, wj, none)], axis=0))
                    rhs.append(jnp.concatenate(
                        [jnp.where(mi == low, wis[i], none), jnp.where(mi == high, wis[i], none)],
                        axis=0))
            return acc + lax.dot_general(
                jnp.concatenate(lhs, axis=1), jnp.concatenate(rhs, axis=1), NT,
                preferred_element_type=jnp.float32)

        steps = (plan_s[height - 1, t] + (UNROLL - 1)) // UNROLL
        acc = lax.fori_loop(0, steps, add_chunk, jnp.zeros((32, 32), jnp.float32))
        r = plan_s[height - 2, t]
        hist_ref[r] = hist_ref[r] + acc
        return carry

    lax.fori_loop(0, plan_s[height - 3, 0], add_tile, 0)


def local(coords, weights, live):
    parts = coords.shape[3]
    slots = lax.iota(jnp.int32, parts)
    own_weight = jnp.where(slots < live[0, 0], weights[0, 0].astype(jnp.float32), 0.0)
    packed = jnp.concatenate(
        [coords.reshape(3, parts).astype(jnp.float32), own_weight.reshape(1, parts)], axis=0
    )
    down, up = shifted(packed, "shell")
    tri = jnp.concatenate([down, packed, up], axis=1)
    total = 3 * parts
    chunks = total // LANES
    own_rows = -(-(parts + SUBREGIONS * (ROWS - 1)) // LANES) * LANES
    vmem = pl.BlockSpec(memory_space=pltpu.VMEM)
    far, own, meta = pl.pallas_call(
        prep_kernel,
        out_shape=(
            jax.ShapeDtypeStruct((chunks, 8, LANES), jnp.float32),
            jax.ShapeDtypeStruct((own_rows, 16), jnp.float32),
            jax.ShapeDtypeStruct((8, LANES), jnp.float32),
        ),
        in_specs=[vmem],
        out_specs=(vmem, vmem, vmem),
        scratch_shapes=[pltpu.VMEM((total, 8), jnp.float32), pltpu.VMEM((parts, 8), jnp.float32)],
    )(tri)
    left, right = shifted(far, "sky")
    every = jnp.concatenate(
        [left, far, right, jnp.zeros((1, 8, LANES), jnp.float32)], axis=0
    )
    height = -(-(3 * chunks + UNROLL + 3) // 8) * 8
    hist = pl.pallas_call(
        pair_kernel,
        out_shape=jax.ShapeDtypeStruct((SUBREGIONS, 32, 32), jnp.float32),
        in_specs=[vmem, vmem, vmem],
        out_specs=vmem,
        scratch_shapes=[
            pltpu.VMEM((height, LANES), jnp.int32),
            pltpu.SMEM((height, LANES), jnp.int32),
            pltpu.SemaphoreType.DMA,
        ],
    )(every, own, meta)
    by_region = hist[:, :S_BINS, :MU_BINS].reshape(SUBREGIONS, S_BINS * MU_BINS)
    sums = lax.all_gather(jnp.sum(by_region, axis=0), "sky")
    shell_total = jnp.sum(sums, axis=0)
    scale = bin_scale(lax.axis_size("sky"))
    leave = (shell_total[None, :] - by_region) * scale[None, :]
    return leave.reshape(1, SUBREGIONS, S_BINS * MU_BINS)


def solution(mesh):
    in_specs = (P(None, "shell", "sky", None), P("shell", "sky", None), P("shell", "sky"))
    out_specs = P("shell", "sky", None)
    return jax.shard_map(local, mesh=mesh, in_specs=in_specs, out_specs=out_specs, check_vma=False)
```

```python
import math

import jax
import jax.numpy as jnp
from jax import lax
from jax.experimental import pallas as pl
from jax.experimental.pallas import tpu as pltpu
from jax.sharding import PartitionSpec as P

PART_DEV = 512
SIDE_CELLS = 256
SPAN_CELLS = 1024
SUBREGIONS = 8
S_BINS = 30
MU_BINS = 20
LANES = 128
ROWS = 8
UNROLL = 8
BIG = 1.0e6
NT = (((1,), (1,)), ((), ()))


def edge_values():
    return [int(4.0 * 10.0 ** (4.0 * level / S_BINS) + 0.5) for level in range(S_BINS + 1)]


REACH = math.isqrt(edge_values()[S_BINS] - 1)


def bin_scale(patches):
    edges = edge_values()
    factor = SIDE_CELLS * SIDE_CELLS * SPAN_CELLS / (patches * PART_DEV * PART_DEV)
    values = []
    for level in range(S_BINS):
        volume = 4.0 * math.pi / 3.0 * (edges[level + 1] ** 1.5 - edges[level] ** 1.5) / MU_BINS
        values = values + [factor / volume] * MU_BINS
    return jnp.asarray(values, dtype=jnp.float32)


def shifted(block, axis):
    count = lax.axis_size(axis)
    forward = [(i, i + 1) for i in range(count - 1)]
    backward = [(target, source) for source, target in forward]
    return lax.ppermute(block, axis, forward), lax.ppermute(block, axis, backward)


def iota_f(shape, dim):
    return lax.broadcasted_iota(jnp.int32, shape, dim).astype(jnp.float32)


def split_rows(x, y, z, w):
    xh, yh, zh = jnp.floor(x * (1 / 64)), jnp.floor(y * (1 / 64)), jnp.floor(z * (1 / 64))
    rows = [xh, yh, zh, w, x - 64 * xh, y - 64 * yh, z - 64 * zh, jnp.where(w > 0, 1.0, 0.0)]
    rows = rows + [jnp.zeros_like(x)] * 8
    return jnp.concatenate(rows, axis=0).astype(jnp.bfloat16)


def prep_kernel(tri_ref, far_ref, own_ref, meta_ref, cols, ocols):
    total = tri_ref.shape[1]
    parts = total // 3
    origin = (lax.axis_index("shell") * SIDE_CELLS).astype(jnp.float32)
    x, y, z, w = (tri_ref[c : c + 1, :] for c in range(4))
    keep = (w > 0) & (x >= origin - REACH) & (x <= origin + (SIDE_CELLS - 1 + REACH))
    wk = jnp.where(keep, w, 0.0)
    key = jnp.where(keep, z, float(SPAN_CELLS)) * total + iota_f((1, total), 1)
    cols[...] = jnp.broadcast_to(key, (8, total)).T

    def count_block(i, rank):
        col = cols[pl.ds(pl.multiple_of(i * LANES, LANES), LANES), 0:1]
        return rank + jnp.sum(jnp.where(col < key, 1.0, 0.0), axis=0, keepdims=True)

    rank = lax.fori_loop(0, total // LANES, count_block, jnp.zeros((1, total), jnp.float32))
    feats = split_rows(x, y, z, wk)

    def place(c, carry):
        dest = iota_f((LANES, total), 0) + (c * LANES).astype(jnp.float32)
        hot = jnp.where(dest == rank, 1.0, 0.0).astype(jnp.bfloat16)
        res = lax.dot_general(feats, hot, NT, preferred_element_type=jnp.float32)
        pos = 64.0 * res[0:3] + res[4:7]
        alive = res[7:8]
        zmin = jnp.min(jnp.where(alive > 0, pos[2:3], BIG), axis=1, keepdims=True)
        zmax = jnp.max(jnp.where(alive > 0, pos[2:3], -BIG), axis=1, keepdims=True)
        some = jnp.max(alive, axis=1, keepdims=True)
        shape = (1, LANES)
        far_ref[c] = jnp.concatenate(
            [pos, res[3:4], jnp.broadcast_to(zmin, shape), jnp.broadcast_to(zmax, shape),
             jnp.broadcast_to(some, shape), alive], axis=0)
        return carry

    lax.fori_loop(0, total // LANES, place, 0)

    mid = slice(parts, 2 * parts)
    x, y, z, w, key = x[:, mid], y[:, mid], z[:, mid], w[:, mid], key[:, mid]
    key_col = cols[parts : 2 * parts, 0:1]
    order = jnp.sum(jnp.where(key_col < key, 1.0, 0.0), axis=0, keepdims=True)
    region = jnp.floor(z * (SUBREGIONS / SPAN_CELLS))
    alive = w > 0
    pos = order
    for r in range(SUBREGIONS - 1):
        count = jnp.sum(jnp.where(alive & (region == r), 1.0, 0.0), axis=1, keepdims=True)
        gap = jnp.floor((count + (ROWS - 1)) * (1 / ROWS)) * ROWS - count
        pos = pos + jnp.where(region > r, gap, 0.0)
    pos = jnp.where(alive, pos, BIG)
    feats = split_rows(x, y, z, w)
    zs = jnp.concatenate([pos, z] + [pos] * 6, axis=0)
    ocols[...] = zs.T

    def place_own(c, carry):
        dest = iota_f((LANES, parts), 0) + (c * LANES).astype(jnp.float32)
        hot = jnp.where(dest == pos, 1.0, 0.0).astype(jnp.bfloat16)
        own_ref[pl.ds(pl.multiple_of(c * LANES, LANES), LANES), :] = lax.dot_general(
            hot, feats, NT, preferred_element_type=jnp.float32)
        return carry

    lax.fori_loop(0, own_ref.shape[0] // LANES, place_own, 0)
    tile = jnp.floor(ocols[:, 0:1] * (1 / ROWS))
    z_col = ocols[:, 1:2]
    mine = tile == iota_f((parts, LANES), 1)
    tmin = jnp.min(jnp.where(mine, z_col, BIG), axis=0, keepdims=True)
    tmax = jnp.max(jnp.where(mine, z_col, -BIG), axis=0, keepdims=True)
    meta_ref[...] = jnp.concatenate([tmin, tmax] + [tmin] * 6, axis=0)


def bins(dx, q):
    per_two = S_BINS / 4.0 * math.log10(2.0)
    cand = jnp.floor(jnp.log2(q) * per_two + (0.5 - 2.0 * per_two))
    edge = jnp.floor(jnp.exp2(cand * (1.0 / per_two) + 2.0) + 0.5)
    s = jnp.where(q < edge, cand - 1.0, cand)
    near = jnp.floor(jnp.abs(dx) * lax.rsqrt(q) * MU_BINS + 0.5)
    m = jnp.where(dx * dx * (MU_BINS * MU_BINS) < near * near * q, near - 1.0, near)
    return s, jnp.minimum(m, MU_BINS - 1.0)


def pair_kernel(far_ref, own_ref, meta_ref, hist_ref, plan_v, plan_s, sem):
    chunks = far_ref.shape[0] - 1
    height = plan_v.shape[0]
    edges = edge_values()
    tmin, tmax = meta_ref[0:1, :], meta_ref[1:2, :]
    slot = lax.broadcasted_iota(jnp.int32, (height, LANES), 0)
    plan = jnp.full((height, LANES), chunks, jnp.int32)
    count = jnp.zeros((1, LANES), jnp.int32)
    for c in range(chunks):
        info = far_ref[c]
        act = (info[4:5] <= tmax + REACH) & (info[5:6] >= tmin - REACH) & (info[6:7] > 0)
        plan = jnp.where((slot == count) & act, c, plan)
        count = count + jnp.where(act, 1, 0)
    region = jnp.clip(jnp.floor(tmin * (SUBREGIONS / SPAN_CELLS)), 0, SUBREGIONS - 1)
    used = jnp.sum(jnp.where(tmin < BIG, 1.0, 0.0), axis=1, keepdims=True)
    plan = jnp.where(slot == height - 1, count, plan)
    plan = jnp.where(slot == height - 2, region.astype(jnp.int32), plan)
    plan = jnp.where(slot == height - 3, used.astype(jnp.int32), plan)
    plan_v[...] = plan
    copy = pltpu.make_async_copy(plan_v, plan_s, sem)
    copy.start()
    hist_ref[...] = jnp.zeros_like(hist_ref)
    copy.wait()

    half = (16, LANES)
    low = iota_f(half, 0).astype(jnp.bfloat16)
    high = (iota_f(half, 0) + 16.0).astype(jnp.bfloat16)
    none = jnp.zeros(half, jnp.bfloat16)

    def add_tile(t, carry):
        own = own_ref[pl.ds(pl.multiple_of(t * ROWS, ROWS), ROWS), :]
        xi = jnp.broadcast_to(own[:, 0:1] * 64.0 + own[:, 4:5], (ROWS, LANES))
        yi = jnp.broadcast_to(own[:, 1:2] * 64.0 + own[:, 5:6], (ROWS, LANES))
        zi = jnp.broadcast_to(own[:, 2:3] * 64.0 + own[:, 6:7], (ROWS, LANES))
        wi = jnp.broadcast_to(own[:, 3:4], (ROWS, LANES))
        wis = [jnp.broadcast_to(wi[i : i + 1], half).astype(jnp.bfloat16) for i in range(ROWS)]

        def add_chunks(first, width, acc):
            lhs, rhs = [], []
            for u in range(width):
                info = far_ref[plan_s[first + u, t]]
                dx, dy, dz = xi - info[0:1], yi - info[1:2], zi - info[2:3]
                q = dx * dx + dy * dy + dz * dz
                s, m = bins(dx, q)
                s = jnp.where((q >= edges[0]) & (q < edges[S_BINS]), s, 99.0)
                wj = jnp.broadcast_to(info[3:4], half).astype(jnp.bfloat16)
                for i in range(ROWS):
                    si = jnp.broadcast_to(s[i : i + 1], half).astype(jnp.bfloat16)
                    mi = jnp.broadcast_to(m[i : i + 1], half).astype(jnp.bfloat16)
                    lhs.append(jnp.concatenate(
                        [jnp.where(si == low, wj, none), jnp.where(si == high, wj, none)], axis=0))
                    rhs.append(jnp.concatenate(
                        [jnp.where(mi == low, wis[i], none), jnp.where(mi == high, wis[i], none)],
                        axis=0))
            return acc + lax.dot_general(
                jnp.concatenate(lhs, axis=1), jnp.concatenate(rhs, axis=1), NT,
                preferred_element_type=jnp.float32)

        count_t = plan_s[height - 1, t]
        short = UNROLL // 2
        steps = (count_t + (short - 1)) // UNROLL
        acc = lax.fori_loop(0, steps, lambda p, acc: add_chunks(p * UNROLL, UNROLL, acc),
                            jnp.zeros((32, 32), jnp.float32))
        done = steps * UNROLL
        acc = lax.fori_loop(0, jnp.where(count_t > done, 1, 0),
                            lambda p, acc: add_chunks(done, short, acc), acc)
        r = plan_s[height - 2, t]
        hist_ref[r] = hist_ref[r] + acc
        return carry

    lax.fori_loop(0, plan_s[height - 3, 0], add_tile, 0)


def local(coords, weights, live):
    parts = coords.shape[3]
    slots = lax.iota(jnp.int32, parts)
    own_weight = jnp.where(slots < live[0, 0], weights[0, 0].astype(jnp.float32), 0.0)
    packed = jnp.concatenate(
        [coords.reshape(3, parts).astype(jnp.float32), own_weight.reshape(1, parts)], axis=0
    )
    down, up = shifted(packed, "shell")
    tri = jnp.concatenate([down, packed, up], axis=1)
    total = 3 * parts
    chunks = total // LANES
    own_rows = -(-(parts + SUBREGIONS * (ROWS - 1)) // LANES) * LANES
    vmem = pl.BlockSpec(memory_space=pltpu.VMEM)
    far, own, meta = pl.pallas_call(
        prep_kernel,
        out_shape=(
            jax.ShapeDtypeStruct((chunks, 8, LANES), jnp.float32),
            jax.ShapeDtypeStruct((own_rows, 16), jnp.float32),
            jax.ShapeDtypeStruct((8, LANES), jnp.float32),
        ),
        in_specs=[vmem],
        out_specs=(vmem, vmem, vmem),
        scratch_shapes=[pltpu.VMEM((total, 8), jnp.float32), pltpu.VMEM((parts, 8), jnp.float32)],
    )(tri)
    left, right = shifted(far, "sky")
    every = jnp.concatenate(
        [left, far, right, jnp.zeros((1, 8, LANES), jnp.float32)], axis=0
    )
    height = -(-(3 * chunks + UNROLL + 3) // 8) * 8
    hist = pl.pallas_call(
        pair_kernel,
        out_shape=jax.ShapeDtypeStruct((SUBREGIONS, 32, 32), jnp.float32),
        in_specs=[vmem, vmem, vmem],
        out_specs=vmem,
        scratch_shapes=[
            pltpu.VMEM((height, LANES), jnp.int32),
            pltpu.SMEM((height, LANES), jnp.int32),
            pltpu.SemaphoreType.DMA,
        ],
    )(every, own, meta)
    by_region = hist[:, :S_BINS, :MU_BINS].reshape(SUBREGIONS, S_BINS * MU_BINS)
    sums = lax.all_gather(jnp.sum(by_region, axis=0), "sky")
    shell_total = jnp.sum(sums, axis=0)
    scale = bin_scale(lax.axis_size("sky"))
    leave = (shell_total[None, :] - by_region) * scale[None, :]
    return leave.reshape(1, SUBREGIONS, S_BINS * MU_BINS)


def solution(mesh):
    in_specs = (P(None, "shell", "sky", None), P("shell", "sky", None), P("shell", "sky"))
    out_specs = P("shell", "sky", None)
    return jax.shard_map(local, mesh=mesh, in_specs=in_specs, out_specs=out_specs, check_vma=False)
```

```python
import math

import jax
import jax.numpy as jnp
from jax import lax
from jax.experimental import pallas as pl
from jax.experimental.pallas import tpu as pltpu
from jax.sharding import PartitionSpec as P

PART_DEV = 512
SIDE_CELLS = 256
SPAN_CELLS = 1024
SUBREGIONS = 8
S_BINS = 30
MU_BINS = 20
LANES = 128
ROWS = 8
UNROLL = 8
BIG = 1.0e6
NT = (((1,), (1,)), ((), ()))


def edge_values():
    return [int(4.0 * 10.0 ** (4.0 * level / S_BINS) + 0.5) for level in range(S_BINS + 1)]


REACH = math.isqrt(edge_values()[S_BINS] - 1)


def bin_scale(patches):
    edges = edge_values()
    factor = SIDE_CELLS * SIDE_CELLS * SPAN_CELLS / (patches * PART_DEV * PART_DEV)
    values = []
    for level in range(S_BINS):
        volume = 4.0 * math.pi / 3.0 * (edges[level + 1] ** 1.5 - edges[level] ** 1.5) / MU_BINS
        values = values + [factor / volume] * MU_BINS
    return jnp.asarray(values, dtype=jnp.float32)


def shifted(block, axis):
    count = lax.axis_size(axis)
    forward = [(i, i + 1) for i in range(count - 1)]
    backward = [(target, source) for source, target in forward]
    return lax.ppermute(block, axis, forward), lax.ppermute(block, axis, backward)


def iota_f(shape, dim):
    return lax.broadcasted_iota(jnp.int32, shape, dim).astype(jnp.float32)


def split_rows(x, y, z, w):
    xh, yh, zh = jnp.floor(x * (1 / 64)), jnp.floor(y * (1 / 64)), jnp.floor(z * (1 / 64))
    rows = [xh, yh, zh, w, x - 64 * xh, y - 64 * yh, z - 64 * zh, jnp.where(w > 0, 1.0, 0.0)]
    rows = rows + [jnp.zeros_like(x)] * 8
    return jnp.concatenate(rows, axis=0).astype(jnp.bfloat16)


def prep_kernel(tri_ref, far_ref, own_ref, meta_ref, cols, ocols):
    total = tri_ref.shape[1]
    parts = total // 3
    origin = (lax.axis_index("shell") * SIDE_CELLS).astype(jnp.float32)
    x, y, z, w = (tri_ref[c : c + 1, :] for c in range(4))
    keep = (w > 0) & (x >= origin - REACH) & (x <= origin + (SIDE_CELLS - 1 + REACH))
    wk = jnp.where(keep, w, 0.0)
    key = jnp.where(keep, z, float(SPAN_CELLS)) * total + iota_f((1, total), 1)
    cols[...] = jnp.broadcast_to(key, (8, total)).T

    def count_block(i, rank):
        col = cols[pl.ds(pl.multiple_of(i * LANES, LANES), LANES), 0:1]
        return rank + jnp.sum(jnp.where(col < key, 1.0, 0.0), axis=0, keepdims=True)

    rank = lax.fori_loop(0, total // LANES, count_block, jnp.zeros((1, total), jnp.float32))
    feats = split_rows(x, y, z, wk)

    def place(c, carry):
        dest = iota_f((LANES, total), 0) + (c * LANES).astype(jnp.float32)
        hot = jnp.where(dest == rank, 1.0, 0.0).astype(jnp.bfloat16)
        res = lax.dot_general(feats, hot, NT, preferred_element_type=jnp.float32)
        pos = 64.0 * res[0:3] + res[4:7]
        alive = res[7:8]
        zmin = jnp.min(jnp.where(alive > 0, pos[2:3], BIG), axis=1, keepdims=True)
        zmax = jnp.max(jnp.where(alive > 0, pos[2:3], -BIG), axis=1, keepdims=True)
        some = jnp.max(alive, axis=1, keepdims=True)
        shape = (1, LANES)
        far_ref[c] = jnp.concatenate(
            [pos, res[3:4], jnp.broadcast_to(zmin, shape), jnp.broadcast_to(zmax, shape),
             jnp.broadcast_to(some, shape), alive], axis=0)
        return carry

    lax.fori_loop(0, total // LANES, place, 0)

    mid = slice(parts, 2 * parts)
    x, y, z, w, key = x[:, mid], y[:, mid], z[:, mid], w[:, mid], key[:, mid]
    key_col = cols[parts : 2 * parts, 0:1]
    order = jnp.sum(jnp.where(key_col < key, 1.0, 0.0), axis=0, keepdims=True)
    region = jnp.floor(z * (SUBREGIONS / SPAN_CELLS))
    alive = w > 0
    pos = order
    for r in range(SUBREGIONS - 1):
        count = jnp.sum(jnp.where(alive & (region == r), 1.0, 0.0), axis=1, keepdims=True)
        gap = jnp.floor((count + (ROWS - 1)) * (1 / ROWS)) * ROWS - count
        pos = pos + jnp.where(region > r, gap, 0.0)
    pos = jnp.where(alive, pos, BIG)
    feats = split_rows(x, y, z, w)
    zs = jnp.concatenate([pos, z] + [pos] * 6, axis=0)
    ocols[...] = zs.T

    def place_own(c, carry):
        dest = iota_f((LANES, parts), 0) + (c * LANES).astype(jnp.float32)
        hot = jnp.where(dest == pos, 1.0, 0.0).astype(jnp.bfloat16)
        own_ref[pl.ds(pl.multiple_of(c * LANES, LANES), LANES), :] = lax.dot_general(
            hot, feats, NT, preferred_element_type=jnp.float32)
        return carry

    lax.fori_loop(0, own_ref.shape[0] // LANES, place_own, 0)
    tile = jnp.floor(ocols[:, 0:1] * (1 / ROWS))
    z_col = ocols[:, 1:2]
    mine = tile == iota_f((parts, LANES), 1)
    tmin = jnp.min(jnp.where(mine, z_col, BIG), axis=0, keepdims=True)
    tmax = jnp.max(jnp.where(mine, z_col, -BIG), axis=0, keepdims=True)
    meta_ref[...] = jnp.concatenate([tmin, tmax] + [tmin] * 6, axis=0)


def bins(dx, q):
    per_two = S_BINS / 4.0 * math.log10(2.0)
    cand = jnp.floor(jnp.log2(q) * per_two + (0.5 - 2.0 * per_two))
    edge = jnp.floor(jnp.exp2(cand * (1.0 / per_two) + 2.0) + 0.5)
    s = jnp.where(q < edge, cand - 1.0, cand)
    near = jnp.floor(jnp.abs(dx) * lax.rsqrt(q) * MU_BINS + 0.5)
    m = jnp.where(dx * dx * (MU_BINS * MU_BINS) < near * near * q, near - 1.0, near)
    return s, jnp.minimum(m, MU_BINS - 1.0)


def pair_kernel(left_ref, mid_ref, right_ref, own_ref, meta_ref, hist_ref, far_ref, plan_v, plan_s, sem):
    chunks = far_ref.shape[0] - 1
    each = mid_ref.shape[0]
    for n, ref in enumerate((left_ref, mid_ref, right_ref)):
        far_ref[n * each : (n + 1) * each] = ref[...]
    far_ref[chunks] = jnp.zeros((8, LANES), jnp.float32)
    height = plan_v.shape[0]
    edges = edge_values()
    tmin, tmax = meta_ref[0:1, :], meta_ref[1:2, :]
    slot = lax.broadcasted_iota(jnp.int32, (height, LANES), 0)
    plan = jnp.full((height, LANES), chunks, jnp.int32)
    count = jnp.zeros((1, LANES), jnp.int32)
    for c in range(chunks):
        info = far_ref[c]
        act = (info[4:5] <= tmax + REACH) & (info[5:6] >= tmin - REACH) & (info[6:7] > 0)
        plan = jnp.where((slot == count) & act, c, plan)
        count = count + jnp.where(act, 1, 0)
    region = jnp.clip(jnp.floor(tmin * (SUBREGIONS / SPAN_CELLS)), 0, SUBREGIONS - 1)
    used = jnp.sum(jnp.where(tmin < BIG, 1.0, 0.0), axis=1, keepdims=True)
    plan = jnp.where(slot == height - 1, count, plan)
    plan = jnp.where(slot == height - 2, region.astype(jnp.int32), plan)
    plan = jnp.where(slot == height - 3, used.astype(jnp.int32), plan)
    plan_v[...] = plan
    copy = pltpu.make_async_copy(plan_v, plan_s, sem)
    copy.start()
    hist_ref[...] = jnp.zeros_like(hist_ref)
    copy.wait()

    half = (16, LANES)
    low = iota_f(half, 0).astype(jnp.bfloat16)
    high = (iota_f(half, 0) + 16.0).astype(jnp.bfloat16)
    none = jnp.zeros(half, jnp.bfloat16)

    def add_tile(t, carry):
        own = own_ref[pl.ds(pl.multiple_of(t * ROWS, ROWS), ROWS), :]
        xi = jnp.broadcast_to(own[:, 0:1] * 64.0 + own[:, 4:5], (ROWS, LANES))
        yi = jnp.broadcast_to(own[:, 1:2] * 64.0 + own[:, 5:6], (ROWS, LANES))
        zi = jnp.broadcast_to(own[:, 2:3] * 64.0 + own[:, 6:7], (ROWS, LANES))
        wi = jnp.broadcast_to(own[:, 3:4], (ROWS, LANES))
        wis = [jnp.broadcast_to(wi[i : i + 1], half).astype(jnp.bfloat16) for i in range(ROWS)]

        def add_chunks(first, width, acc):
            lhs, rhs = [], []
            for u in range(width):
                info = far_ref[plan_s[first + u, t]]
                dx, dy, dz = xi - info[0:1], yi - info[1:2], zi - info[2:3]
                q = dx * dx + dy * dy + dz * dz
                s, m = bins(dx, q)
                s = jnp.where((q >= edges[0]) & (q < edges[S_BINS]), s, 99.0)
                wj = jnp.broadcast_to(info[3:4], half).astype(jnp.bfloat16)
                for i in range(ROWS):
                    si = jnp.broadcast_to(s[i : i + 1], half).astype(jnp.bfloat16)
                    mi = jnp.broadcast_to(m[i : i + 1], half).astype(jnp.bfloat16)
                    lhs.append(jnp.concatenate(
                        [jnp.where(si == low, wj, none), jnp.where(si == high, wj, none)], axis=0))
                    rhs.append(jnp.concatenate(
                        [jnp.where(mi == low, wis[i], none), jnp.where(mi == high, wis[i], none)],
                        axis=0))
            return acc + lax.dot_general(
                jnp.concatenate(lhs, axis=1), jnp.concatenate(rhs, axis=1), NT,
                preferred_element_type=jnp.float32)

        count_t = plan_s[height - 1, t]
        short = UNROLL // 2
        steps = (count_t + (short - 1)) // UNROLL
        acc = lax.fori_loop(0, steps, lambda p, acc: add_chunks(p * UNROLL, UNROLL, acc),
                            jnp.zeros((32, 32), jnp.float32))
        done = steps * UNROLL
        acc = lax.fori_loop(0, jnp.where(count_t > done, 1, 0),
                            lambda p, acc: add_chunks(done, short, acc), acc)
        r = plan_s[height - 2, t]
        hist_ref[r] = hist_ref[r] + acc
        return carry

    lax.fori_loop(0, plan_s[height - 3, 0], add_tile, 0)


def local(coords, weights, live):
    parts = coords.shape[3]
    slots = lax.iota(jnp.int32, parts)
    own_weight = jnp.where(slots < live[0, 0], weights[0, 0].astype(jnp.float32), 0.0)
    packed = jnp.concatenate(
        [coords.reshape(3, parts).astype(jnp.float32), own_weight.reshape(1, parts)], axis=0
    )
    down, up = shifted(packed, "shell")
    tri = jnp.concatenate([down, packed, up], axis=1)
    total = 3 * parts
    chunks = total // LANES
    own_rows = -(-(parts + SUBREGIONS * (ROWS - 1)) // LANES) * LANES
    vmem = pl.BlockSpec(memory_space=pltpu.VMEM)
    far, own, meta = pl.pallas_call(
        prep_kernel,
        out_shape=(
            jax.ShapeDtypeStruct((chunks, 8, LANES), jnp.float32),
            jax.ShapeDtypeStruct((own_rows, 16), jnp.float32),
            jax.ShapeDtypeStruct((8, LANES), jnp.float32),
        ),
        in_specs=[vmem],
        out_specs=(vmem, vmem, vmem),
        scratch_shapes=[pltpu.VMEM((total, 8), jnp.float32), pltpu.VMEM((parts, 8), jnp.float32)],
    )(tri)
    left, right = shifted(far, "sky")
    height = -(-(3 * chunks + UNROLL + 3) // 8) * 8
    hist = pl.pallas_call(
        pair_kernel,
        out_shape=jax.ShapeDtypeStruct((SUBREGIONS, 32, 32), jnp.float32),
        in_specs=[vmem] * 5,
        out_specs=vmem,
        scratch_shapes=[
            pltpu.VMEM((3 * chunks + 1, 8, LANES), jnp.float32),
            pltpu.VMEM((height, LANES), jnp.int32),
            pltpu.SMEM((height, LANES), jnp.int32),
            pltpu.SemaphoreType.DMA,
        ],
    )(left, far, right, own, meta)
    by_region = hist[:, :S_BINS, :MU_BINS].reshape(SUBREGIONS, S_BINS * MU_BINS)
    sums = lax.all_gather(jnp.sum(by_region, axis=0), "sky")
    shell_total = jnp.sum(sums, axis=0)
    scale = bin_scale(lax.axis_size("sky"))
    leave = (shell_total[None, :] - by_region) * scale[None, :]
    return leave.reshape(1, SUBREGIONS, S_BINS * MU_BINS)


def solution(mesh):
    in_specs = (P(None, "shell", "sky", None), P("shell", "sky", None), P("shell", "sky"))
    out_specs = P("shell", "sky", None)
    return jax.shard_map(local, mesh=mesh, in_specs=in_specs, out_specs=out_specs, check_vma=False)
```
